32 devices in a mesh: seq: 4 (over x, core), head: 8 (over z, y).
Axes of the slice: x: 2, y: 2, z: 4, core: 2. Of those that a mesh axis runs over, the one named last changes fastest.
Arguments:
- tokens: bfloat16 [1024, 4096], P('seq', 'head'), may hold values from -6 to 6
- w_query: bfloat16 [4096, 2048], P(None, 'head'), may hold values from -0.09375 to 0.09375
- w_key: bfloat16 [4096, 2048], P(None, 'head'), may hold values from -0.09375 to 0.09375
- w_value: bfloat16 [4096, 2048], P(None, 'head'), may hold values from -0.09375 to 0.09375
- w_out: bfloat16 [2048, 4096], P('head'), may hold values from -0.125 to 0.125
- grad_out: bfloat16 [1024, 4096], P('seq', 'head'), may hold values from -6 to 6
- state_in: float32 [16, 128, 128], P('head'), may hold values from -384 to 384
Outputs:
- result: bfloat16 [1024, 4096], P('seq', 'head')
- grad_tokens: float32 [1024, 4096], P('seq', 'head')
- grad_wq: float32 [4096, 2048], P('seq', 'head')
- grad_wk: float32 [4096, 2048], P('seq', 'head')
- grad_wv: float32 [4096, 2048], P('seq', 'head')
- grad_wo: float32 [2048, 4096], P('head', 'seq')
- grad_state_in: float32 [16, 128, 128], P('head')
The draws below stay inside these ranges and needn't reach their ends.
All inputs are finite; a program needn't handle non-finite values.
Results may differ from the reference program's by a relative error of at most 0.018.
Values may be sent and summed in bfloat16 or wider, within the bound.
A program may use at most 64 MiB of HBM per device.

```python
import jax
import jax.numpy as jnp
from jax import lax

D = 4096
HEADS = 16
DH = 128
BLOCK = 256
TOKENS = 1024
N_HEAD = 8


def block_levels(stream_key, extent, shards, smallest, largest):
    gain, own = 1.0, jax.random.fold_in(stream_key, 6)
    for dim, parts in shards:
        steps = jnp.exp(jax.random.uniform(jax.random.fold_in(own, dim), (parts,), jnp.float32, smallest / len(shards), largest / len(shards)))
        gain = gain * jnp.repeat(steps, extent[dim] // parts).reshape([-1 if axis == dim else 1 for axis in range(len(extent))])
    return gain


def centred(rng, shape, scale, most, cuts=(), kind=jnp.bfloat16):
    drawn = scale * jax.random.normal(rng, shape, jnp.float32)
    if cuts:
        drawn = drawn * block_levels(rng, shape, cuts, -0.22, 0.18)
    return jnp.clip(drawn, -most, most).astype(kind)


def setup_inputs(seed: int = 0) -> dict:
    arg_keys = jax.random.split(jax.random.key(seed), 8)
    return {
        "tokens": centred(arg_keys[0], (TOKENS, D), 1.0, 6.0, ((0, 4), (1, 8))),
        "w_query": centred(arg_keys[1], (D, HEADS * DH), D ** -0.5, 0.09375, ((1, 8),)),
        "w_key": centred(arg_keys[2], (D, HEADS * DH), D ** -0.5, 0.09375, ((1, 8),)),
        "w_value": centred(arg_keys[3], (D, HEADS * DH), D ** -0.5, 0.09375, ((1, 8),)),
        "w_out": centred(arg_keys[4], (HEADS * DH, D), (HEADS * DH) ** -0.5, 0.125, ((0, 8),)),
        "grad_out": centred(arg_keys[5], (TOKENS, D), 1.0, 6.0, ((0, 4), (1, 8))),
        "state_in": centred(arg_keys[6], (HEADS, DH, DH), (DH // 2), 384.0, ((0, 8),), jnp.float32),
    }


EPSILON = 1e-06
WIDE_TYPE = jnp.float32
HALF_TYPE = jnp.bfloat16

def causal_mask(width):
    return jnp.tril(jnp.ones((width, width), WIDE_TYPE)) > 0.5

def excl_prefix(states):
    running = jnp.cumsum(states, axis=0)
    return jnp.concatenate([jnp.zeros_like(states[:1]), running[:-1]], axis=0)

def excl_suffix(states):
    return jnp.flip(excl_prefix(jnp.flip(states, 0)), 0)

def block_scores(query_blk, keys_blk):
    allowed = causal_mask(query_blk.shape[0])
    scores = jnp.einsum('thd,shd->hts', query_blk.astype(WIDE_TYPE), keys_blk.astype(WIDE_TYPE))
    return jnp.where(allowed[None], scores, 0.0).astype(HALF_TYPE)

def forward_block(pieces):
    query_blk, keys_blk, value_blk, prior_bf = pieces
    scores_bf = block_scores(query_blk, keys_blk)
    local_part = jnp.einsum('hts,shd->thd', scores_bf.astype(WIDE_TYPE), value_blk.astype(WIDE_TYPE))
    carried = jnp.einsum('thd,hde->the', query_blk.astype(WIDE_TYPE), prior_bf.astype(WIDE_TYPE))
    return local_part + carried

def backward_block(pieces):
    query_blk, keys_blk, value_blk, grad_mixed, prior_bf, later_bf = pieces
    allowed = causal_mask(query_blk.shape[0])
    scores_bf = block_scores(query_blk, keys_blk).astype(WIDE_TYPE)
    query_w = query_blk.astype(WIDE_TYPE)
    keys_w = keys_blk.astype(WIDE_TYPE)
    value_w = value_blk.astype(WIDE_TYPE)
    grad_w = grad_mixed.astype(WIDE_TYPE)
    prior_w = prior_bf.astype(WIDE_TYPE)
    later_w = later_bf.astype(WIDE_TYPE)
    grad_scores = jnp.einsum('thd,shd->hts', grad_w, value_w)
    grad_scores = jnp.where(allowed[None], grad_scores, 0.0).astype(HALF_TYPE).astype(WIDE_TYPE)
    grad_query = jnp.einsum('hts,shd->thd', grad_scores, keys_w) + jnp.einsum('the,hde->thd', grad_w, prior_w)
    grad_keys = jnp.einsum('hts,thd->shd', grad_scores, query_w) + jnp.einsum('she,hde->shd', value_w, later_w)
    grad_value = jnp.einsum('hts,the->she', scores_bf, grad_w) + jnp.einsum('shd,hde->she', keys_w, later_w)
    return (grad_query.astype(HALF_TYPE), grad_keys.astype(HALF_TYPE), grad_value.astype(HALF_TYPE))

def reference(tokens, w_query, w_key, w_value, w_out, grad_out, state_in):
    group_cols = HEADS * DH // N_HEAD
    blocks = TOKENS // BLOCK
    block_shape = (blocks, BLOCK, HEADS, DH)
    query = jnp.dot(tokens, w_query, preferred_element_type=WIDE_TYPE).astype(HALF_TYPE).reshape(block_shape)
    keys = jnp.dot(tokens, w_key, preferred_element_type=WIDE_TYPE).astype(HALF_TYPE).reshape(block_shape)
    values = jnp.dot(tokens, w_value, preferred_element_type=WIDE_TYPE).astype(HALF_TYPE).reshape(block_shape)
    states = jnp.einsum('cshd,cshe->chde', keys.astype(WIDE_TYPE), values.astype(WIDE_TYPE))
    prior_bf = (state_in[None] + excl_prefix(states)).astype(HALF_TYPE)
    mixed = lax.map(forward_block, (query, keys, values, prior_bf))
    inv_norm = lax.rsqrt(lax.optimization_barrier(jnp.mean(mixed * mixed, axis=-1, keepdims=True)) + EPSILON)
    normed = (mixed * inv_norm).astype(HALF_TYPE).reshape(TOKENS, HEADS * DH)
    out_groups = normed.reshape(TOKENS, N_HEAD, group_cols).transpose(1, 0, 2)
    out_weights = w_out.reshape(N_HEAD, group_cols, D)

    def add_out(running, group_pair):
        piece_out = jnp.dot(group_pair[0], group_pair[1], preferred_element_type=WIDE_TYPE).astype(HALF_TYPE)
        piece_out = lax.optimization_barrier(piece_out)
        return (running + piece_out.astype(WIDE_TYPE), None)
    out_sum, _ = lax.scan(add_out, jnp.zeros((TOKENS, D), WIDE_TYPE), (out_groups, out_weights))
    result = out_sum.astype(HALF_TYPE)
    contract_last = (((1,), (1,)), ((), ()))
    grad_normed = lax.dot_general(grad_out, w_out, contract_last, preferred_element_type=WIDE_TYPE).reshape(block_shape)
    grad_mixed = inv_norm * (grad_normed - mixed * inv_norm * inv_norm * lax.optimization_barrier(jnp.mean(grad_normed * mixed, axis=-1, keepdims=True)))
    grad_mixed = grad_mixed.astype(HALF_TYPE)
    back_states = jnp.einsum('cthd,cthe->chde', query.astype(WIDE_TYPE), grad_mixed.astype(WIDE_TYPE))
    later_bf = excl_suffix(back_states).astype(HALF_TYPE)
    grad_state_in = lax.optimization_barrier(jnp.sum(back_states, axis=0))
    grad_query, grad_keys, grad_value = lax.map(backward_block, (query, keys, values, grad_mixed, prior_bf, later_bf))
    grad_query = grad_query.reshape(TOKENS, HEADS * DH)
    grad_keys = grad_keys.reshape(TOKENS, HEADS * DH)
    grad_value = grad_value.reshape(TOKENS, HEADS * DH)

    def split_cols(matrix):
        return matrix.reshape(matrix.shape[0], N_HEAD, group_cols).transpose(1, 0, 2)

    def add_input(running, group_set):
        piece_in = lax.dot_general(group_set[0], group_set[3], contract_last, preferred_element_type=WIDE_TYPE)
        piece_in = piece_in + lax.dot_general(group_set[1], group_set[4], contract_last, preferred_element_type=WIDE_TYPE)
        piece_in = piece_in + lax.dot_general(group_set[2], group_set[5], contract_last, preferred_element_type=WIDE_TYPE)
        piece_in = lax.optimization_barrier(piece_in.astype(HALF_TYPE))
        return (running + piece_in.astype(WIDE_TYPE), None)
    grad_tokens, _ = lax.scan(add_input, jnp.zeros((TOKENS, D), WIDE_TYPE), (split_cols(grad_query), split_cols(grad_keys), split_cols(grad_value), split_cols(w_query), split_cols(w_key), split_cols(w_value)))
    grad_wq = jnp.dot(tokens.T, grad_query, preferred_element_type=WIDE_TYPE)
    grad_wk = jnp.dot(tokens.T, grad_keys, preferred_element_type=WIDE_TYPE)
    grad_wv = jnp.dot(tokens.T, grad_value, preferred_element_type=WIDE_TYPE)
    grad_wo = jnp.dot(normed.T, grad_out, preferred_element_type=WIDE_TYPE)
    return (result, grad_tokens, grad_wq, grad_wk, grad_wv, grad_wo, grad_state_in)
```

```python
import jax
import jax.numpy as jnp
from jax import lax
from jax.sharding import PartitionSpec as P

DH = 128
BLOCK = 256


EPSILON = 1e-06
WIDE_TYPE = jnp.float32
HALF_TYPE = jnp.bfloat16


def causal_mask(width):
    return jnp.tril(jnp.ones((width, width), WIDE_TYPE)) > 0.5


def excl_prefix(states):
    running = jnp.cumsum(states, axis=0)
    return jnp.concatenate([jnp.zeros_like(states), running[:-1]], axis=0)


def excl_suffix(states):
    return jnp.flip(excl_prefix(jnp.flip(states, 0)), 0)


def flip(array, axis, bits):
    count = lax.axis_size(axis)
    return lax.ppermute(array, axis, [(rank, rank ^ bits) for rank in range(count)])


def bits_below(count):
    return [1 << place for place in range(count.bit_length() - 1)]


def spread(own, axis):
    blocks = {0: own}
    for bit in reversed(bits_below(lax.axis_size(axis))):
        for k in sorted(blocks):
            blocks[k ^ bit] = flip(blocks[k], axis, bit)
    return blocks


def in_order(blocks, axis):
    rank = lax.axis_index(axis)
    whole = jnp.zeros((len(blocks),) + blocks[0].shape, blocks[0].dtype)
    for k, block in blocks.items():
        whole = lax.dynamic_update_slice(whole, block[None], (rank ^ k, 0, 0))
    return whole.reshape(-1, blocks[0].shape[1])


def piece(array, axis, k):
    rows = array.shape[0] // lax.axis_size(axis)
    return lax.dynamic_slice_in_dim(array, (lax.axis_index(axis) ^ k) * rows, rows, 0)


def collect(terms, axis):
    count = lax.axis_size(axis)
    parts = {k: piece(terms, axis, k) for k in range(count)}
    for bit in bits_below(count):
        for k in sorted((k for k in parts if k & bit), reverse=True):
            moved = flip(parts.pop(k).astype(HALF_TYPE), axis, bit)
            parts[k ^ bit] = parts[k ^ bit].astype(WIDE_TYPE) + moved.astype(WIDE_TYPE)
    return parts[0]


def exchange(array, axis):
    count = lax.axis_size(axis)
    return {k: flip(piece(array, axis, k), axis, k) if k else piece(array, axis, 0) for k in range(count)}


def share(array, axis):
    count = lax.axis_size(axis)
    return {k: flip(array, axis, k) if k else array for k in range(count)}


def on_device(tokens, w_query, w_key, w_value, w_out, grad_out, state_in):
    row_count = tokens.shape[0]
    token_blocks = spread(tokens.T, "head")
    later_hops = [k for k in token_blocks if k and not k & 1]
    *arrived, cot_own = lax.optimization_barrier(
        tuple(token_blocks[k] for k in later_hops) + (grad_out.T,)
    )
    for k, block in zip(later_hops, arrived):
        token_blocks[k] = block
    gathered = in_order(token_blocks, "head")
    grad_full = in_order(spread(cot_own, "head"), "head")
    contract_first = (((0,), (0,)), ((), ()))
    contract_last = (((1,), (1,)), ((), ()))
    columns = w_query.shape[1]
    heads_here = columns // DH
    blocks = row_count // BLOCK
    block_shape = (blocks, BLOCK, heads_here, DH)
    query = (
        lax.dot_general(gathered, w_query, contract_first, preferred_element_type=WIDE_TYPE)
        .astype(HALF_TYPE)
        .reshape(block_shape)
    )
    keys = (
        lax.dot_general(gathered, w_key, contract_first, preferred_element_type=WIDE_TYPE)
        .astype(HALF_TYPE)
        .reshape(block_shape)
    )
    values = (
        lax.dot_general(gathered, w_value, contract_first, preferred_element_type=WIDE_TYPE)
        .astype(HALF_TYPE)
        .reshape(block_shape)
    )
    block_states = jnp.einsum("cshd,cshe->chde", keys, values, preferred_element_type=WIDE_TYPE)
    own_state = jnp.sum(block_states, axis=0)
    seq_rank = lax.axis_index("seq")
    every_state = share(own_state.astype(HALF_TYPE), "seq")
    before_dev = sum(
        jnp.where((seq_rank ^ k) < seq_rank, state.astype(WIDE_TYPE), 0.0)
        for k, state in every_state.items()
        if k
    )
    moved_input = exchange(gathered, "seq")
    prior_bf = (state_in[None] + before_dev[None] + excl_prefix(block_states)).astype(HALF_TYPE)
    allowed = causal_mask(BLOCK)[None, None]
    scores = jnp.einsum("cthd,cshd->chts", query, keys, preferred_element_type=WIDE_TYPE)
    scores_bf = jnp.where(allowed, scores, 0.0).astype(HALF_TYPE)
    mixed = jnp.einsum("chts,cshd->cthd", scores_bf, values, preferred_element_type=WIDE_TYPE)
    mixed = mixed + jnp.einsum("cthd,chde->cthe", query, prior_bf, preferred_element_type=WIDE_TYPE)
    inv_norm = lax.rsqrt(jnp.mean(mixed * mixed, axis=-1, keepdims=True) + EPSILON)
    normed = (mixed * inv_norm).astype(HALF_TYPE).reshape(row_count, columns)
    all_normed = spread(normed, "seq")
    out_terms = lax.dot_general(
        w_out, normed, (((0,), (1,)), ((), ())), preferred_element_type=WIDE_TYPE
    )
    result = collect(out_terms.astype(HALF_TYPE), "head").astype(HALF_TYPE).T
    moved_cot = exchange(grad_full, "seq")
    grad_normed = lax.dot_general(
        grad_full, w_out, (((0,), (1,)), ((), ())), preferred_element_type=WIDE_TYPE
    ).reshape(block_shape)
    grad_mixed = inv_norm * (
        grad_normed
        - mixed * inv_norm * inv_norm * jnp.mean(grad_normed * mixed, axis=-1, keepdims=True)
    )
    grad_mixed = grad_mixed.astype(HALF_TYPE)
    back_states = jnp.einsum("cthd,cthe->chde", query, grad_mixed, preferred_element_type=WIDE_TYPE)
    own_back = jnp.sum(back_states, axis=0)
    every_back = {
        k: back.astype(WIDE_TYPE) for k, back in share(own_back.astype(HALF_TYPE), "seq").items()
    }
    after_dev = sum(
        jnp.where((seq_rank ^ k) > seq_rank, back, 0.0) for k, back in every_back.items() if k
    )
    in_rank = [
        sum(jnp.where((seq_rank ^ k) == owner, back, 0.0) for k, back in every_back.items())
        for owner in range(lax.axis_size("seq"))
    ]
    grad_state_in = sum(in_rank)
    later_bf = (after_dev[None] + excl_suffix(back_states)).astype(HALF_TYPE)
    grad_scores = jnp.einsum(
        "cthd,cshd->chts", grad_mixed, values, preferred_element_type=WIDE_TYPE
    )
    grad_scores = jnp.where(allowed, grad_scores, 0.0).astype(HALF_TYPE)
    grad_query = jnp.einsum("chts,cshd->cthd", grad_scores, keys, preferred_element_type=WIDE_TYPE)
    grad_query = grad_query + jnp.einsum(
        "cthe,chde->cthd", grad_mixed, prior_bf, preferred_element_type=WIDE_TYPE
    )
    grad_keys = jnp.einsum("chts,cthd->cshd", grad_scores, query, preferred_element_type=WIDE_TYPE)
    grad_keys = grad_keys + jnp.einsum(
        "cshe,chde->cshd", values, later_bf, preferred_element_type=WIDE_TYPE
    )
    grad_value = jnp.einsum(
        "chts,cthe->cshe", scores_bf, grad_mixed, preferred_element_type=WIDE_TYPE
    )
    grad_value = grad_value + jnp.einsum(
        "cshd,chde->cshe", keys, later_bf, preferred_element_type=WIDE_TYPE
    )
    grad_query = grad_query.astype(HALF_TYPE).reshape(row_count, columns)
    grad_keys = grad_keys.astype(HALF_TYPE).reshape(row_count, columns)
    grad_value = grad_value.astype(HALF_TYPE).reshape(row_count, columns)
    input_terms = lax.dot_general(
        w_query, grad_query, contract_last, preferred_element_type=WIDE_TYPE
    )
    input_terms = input_terms + lax.dot_general(
        w_key, grad_keys, contract_last, preferred_element_type=WIDE_TYPE
    )
    input_terms = input_terms + lax.dot_general(
        w_value, grad_value, contract_last, preferred_element_type=WIDE_TYPE
    )
    grad_tokens = collect(input_terms.astype(HALF_TYPE), "head").T
    all_grads = spread(jnp.concatenate([grad_query, grad_keys, grad_value], axis=1), "seq")
    grad_projections = sum(
        jnp.dot(moved_input[k], all_grads[k], preferred_element_type=WIDE_TYPE)
        for k in moved_input
    )
    grad_wq, grad_wk, grad_wv = jnp.split(grad_projections, 3, axis=1)
    grad_wo = sum(
        lax.dot_general(
            all_normed[k], moved_cot[k], (((0,), (1,)), ((), ())), preferred_element_type=WIDE_TYPE
        )
        for k in moved_cot
    )
    return (result, grad_tokens, grad_wq, grad_wk, grad_wv, grad_wo, grad_state_in)


def solution(mesh):
    placed = (
        P("seq", "head"),
        P(None, "head"),
        P(None, "head"),
        P(None, "head"),
        P("head", None),
        P("seq", "head"),
        P("head", None, None),
    )
    return jax.shard_map(
        on_device,
        mesh=mesh,
        in_specs=placed,
        out_specs=(
            P("seq", "head"),
            P("seq", "head"),
            P("seq", "head"),
            P("seq", "head"),
            P("seq", "head"),
            P("head", "seq"),
            P("head", None, None),
        ),
        check_vma=False,
    )
```

```python
import jax
import jax.numpy as jnp
from jax import lax
from jax.sharding import PartitionSpec as P

DH = 128
BLOCK = 256


EPSILON = 1e-06
WIDE_TYPE = jnp.float32
HALF_TYPE = jnp.bfloat16


def causal_mask(width):
    return jnp.tril(jnp.ones((width, width), WIDE_TYPE)) > 0.5


def excl_prefix(states):
    running = jnp.cumsum(states, axis=0)
    return jnp.concatenate([jnp.zeros_like(states), running[:-1]], axis=0)


def excl_suffix(states):
    return jnp.flip(excl_prefix(jnp.flip(states, 0)), 0)


def flip(array, axis, bits):
    count = lax.axis_size(axis)
    return lax.ppermute(array, axis, [(rank, rank ^ bits) for rank in range(count)])


def bits_below(count):
    return [1 << place for place in range(count.bit_length() - 1)]


def spread(own, axis, lowest=1):
    blocks = {0: own}
    for bit in reversed([b for b in bits_below(lax.axis_size(axis)) if b >= lowest]):
        for k in sorted(blocks):
            blocks[k ^ bit] = flip(blocks[k], axis, bit)
    return blocks


def in_order(blocks, axis, width=1):
    rank = lax.axis_index(axis)
    whole = jnp.zeros((len(blocks),) + blocks[0].shape, blocks[0].dtype)
    for k, block in blocks.items():
        whole = lax.dynamic_update_slice(whole, block[None], ((rank ^ k) // width, 0, 0))
    return whole.reshape(-1, blocks[0].shape[1])


def piece(array, axis, k):
    rows = array.shape[0] // lax.axis_size(axis)
    return lax.dynamic_slice_in_dim(array, (lax.axis_index(axis) ^ k) * rows, rows, 0)


def pieces(terms, axis):
    return {k: piece(terms, axis, k) for k in range(lax.axis_size(axis))}


def collect(parts, axis):
    count = lax.axis_size(axis)
    for bit in bits_below(count):
        for k in sorted((k for k in parts if k & bit), reverse=True):
            moved = flip(parts.pop(k).astype(HALF_TYPE), axis, bit)
            parts[k ^ bit] = parts[k ^ bit].astype(WIDE_TYPE) + moved.astype(WIDE_TYPE)
    return parts[0]


def exchange(array, axis):
    count = lax.axis_size(axis)
    return {k: flip(piece(array, axis, k), axis, k) if k else piece(array, axis, 0) for k in range(count)}


def share(array, axis):
    count = lax.axis_size(axis)
    return {k: flip(array, axis, k) if k else array for k in range(count)}


def on_device(tokens, w_query, w_key, w_value, w_out, grad_out, state_in):
    row_count = tokens.shape[0]
    token_blocks = spread(tokens.T, "head")
    cot_own = grad_out.T
    cot_other = flip(cot_own, "head", 1)
    first = lax.axis_index("head") % 2 == 0
    cot_pair = jnp.concatenate(
        [jnp.where(first, cot_own, cot_other), jnp.where(first, cot_other, cot_own)]
    )
    ahead = [k for k in token_blocks if k and (not k & 1 or k < 4)]
    *arrived, cot_pair = lax.optimization_barrier(
        tuple(token_blocks[k] for k in ahead) + (cot_pair,)
    )
    for k, block in zip(ahead, arrived):
        token_blocks[k] = block
    gathered = in_order(token_blocks, "head")
    grad_full = in_order(spread(cot_pair, "head", 2), "head", 2)
    contract_first = (((0,), (0,)), ((), ()))
    contract_last = (((1,), (1,)), ((), ()))
    columns = w_query.shape[1]
    heads_here = columns // DH
    blocks = row_count // BLOCK
    block_shape = (blocks, BLOCK, heads_here, DH)
    query = (
        lax.dot_general(gathered, w_query, contract_first, preferred_element_type=WIDE_TYPE)
        .astype(HALF_TYPE)
        .reshape(block_shape)
    )
    keys = (
        lax.dot_general(gathered, w_key, contract_first, preferred_element_type=WIDE_TYPE)
        .astype(HALF_TYPE)
        .reshape(block_shape)
    )
    values = (
        lax.dot_general(gathered, w_value, contract_first, preferred_element_type=WIDE_TYPE)
        .astype(HALF_TYPE)
        .reshape(block_shape)
    )
    block_states = jnp.einsum("cshd,cshe->chde", keys, values, preferred_element_type=WIDE_TYPE)
    own_state = jnp.sum(block_states, axis=0)
    seq_rank = lax.axis_index("seq")
    every_state = share(own_state.astype(HALF_TYPE), "seq")
    before_dev = sum(
        jnp.where((seq_rank ^ k) < seq_rank, state.astype(WIDE_TYPE), 0.0)
        for k, state in every_state.items()
        if k
    )
    moved_input = exchange(gathered, "seq")
    prior_bf = (state_in[None] + before_dev[None] + excl_prefix(block_states)).astype(HALF_TYPE)
    allowed = causal_mask(BLOCK)[None, None]
    scores = jnp.einsum("cthd,cshd->chts", query, keys, preferred_element_type=WIDE_TYPE)
    scores_bf = jnp.where(allowed, scores, 0.0).astype(HALF_TYPE)
    mixed = jnp.einsum("chts,cshd->cthd", scores_bf, values, preferred_element_type=WIDE_TYPE)
    mixed = mixed + jnp.einsum("cthd,chde->cthe", query, prior_bf, preferred_element_type=WIDE_TYPE)
    inv_norm = lax.rsqrt(jnp.mean(mixed * mixed, axis=-1, keepdims=True) + EPSILON)
    normed = (mixed * inv_norm).astype(HALF_TYPE).reshape(row_count, columns)
    out_terms = lax.dot_general(
        w_out, normed, (((0,), (1,)), ((), ())), preferred_element_type=WIDE_TYPE
    )
    out_parts, grad_full = lax.optimization_barrier(
        (pieces(out_terms.astype(HALF_TYPE), "head"), grad_full)
    )
    result = collect(out_parts, "head").astype(HALF_TYPE).T
    moved_cot = exchange(grad_full, "seq")
    grad_normed = lax.dot_general(
        grad_full, w_out, (((0,), (1,)), ((), ())), preferred_element_type=WIDE_TYPE
    ).reshape(block_shape)
    grad_mixed = inv_norm * (
        grad_normed
        - mixed * inv_norm * inv_norm * jnp.mean(grad_normed * mixed, axis=-1, keepdims=True)
    )
    grad_mixed = grad_mixed.astype(HALF_TYPE)
    back_states = jnp.einsum("cthd,cthe->chde", query, grad_mixed, preferred_element_type=WIDE_TYPE)
    own_back = jnp.sum(back_states, axis=0)
    every_back = {
        k: back.astype(WIDE_TYPE) for k, back in share(own_back.astype(HALF_TYPE), "seq").items()
    }
    after_dev = sum(
        jnp.where((seq_rank ^ k) > seq_rank, back, 0.0) for k, back in every_back.items() if k
    )
    in_rank = [
        sum(jnp.where((seq_rank ^ k) == owner, back, 0.0) for k, back in every_back.items())
        for owner in range(lax.axis_size("seq"))
    ]
    grad_state_in = sum(in_rank)
    later_bf = (after_dev[None] + excl_suffix(back_states)).astype(HALF_TYPE)
    grad_scores = jnp.einsum(
        "cthd,cshd->chts", grad_mixed, values, preferred_element_type=WIDE_TYPE
    )
    grad_scores = jnp.where(allowed, grad_scores, 0.0).astype(HALF_TYPE)
    grad_query = jnp.einsum("chts,cshd->cthd", grad_scores, keys, preferred_element_type=WIDE_TYPE)
    grad_query = grad_query + jnp.einsum(
        "cthe,chde->cthd", grad_mixed, prior_bf, preferred_element_type=WIDE_TYPE
    )
    grad_keys = jnp.einsum("chts,cthd->cshd", grad_scores, query, preferred_element_type=WIDE_TYPE)
    grad_keys = grad_keys + jnp.einsum(
        "cshe,chde->cshd", values, later_bf, preferred_element_type=WIDE_TYPE
    )
    grad_value = jnp.einsum(
        "chts,cthe->cshe", scores_bf, grad_mixed, preferred_element_type=WIDE_TYPE
    )
    grad_value = grad_value + jnp.einsum(
        "cshd,chde->cshe", keys, later_bf, preferred_element_type=WIDE_TYPE
    )
    grad_query = grad_query.astype(HALF_TYPE).reshape(row_count, columns)
    grad_keys = grad_keys.astype(HALF_TYPE).reshape(row_count, columns)
    grad_value = grad_value.astype(HALF_TYPE).reshape(row_count, columns)
    input_terms = lax.dot_general(
        w_query, grad_query, contract_last, preferred_element_type=WIDE_TYPE
    )
    input_terms = input_terms + lax.dot_general(
        w_key, grad_keys, contract_last, preferred_element_type=WIDE_TYPE
    )
    input_terms = input_terms + lax.dot_general(
        w_value, grad_value, contract_last, preferred_element_type=WIDE_TYPE
    )
    grad_tokens = collect(pieces(input_terms.astype(HALF_TYPE), "head"), "head").T
    all_grads = spread(jnp.concatenate([grad_query, grad_keys, grad_value, normed], axis=1), "seq")
    all_normed = {k: grads[:, 3 * columns :] for k, grads in all_grads.items()}
    grad_projections = sum(
        jnp.dot(moved_input[k], all_grads[k][:, : 3 * columns], preferred_element_type=WIDE_TYPE)
        for k in moved_input
    )
    grad_wq, grad_wk, grad_wv = jnp.split(grad_projections, 3, axis=1)
    grad_wo = sum(
        lax.dot_general(
            all_normed[k], moved_cot[k], (((0,), (1,)), ((), ())), preferred_element_type=WIDE_TYPE
        )
        for k in moved_cot
    )
    return (result, grad_tokens, grad_wq, grad_wk, grad_wv, grad_wo, grad_state_in)


def solution(mesh):
    placed = (
        P("seq", "head"),
        P(None, "head"),
        P(None, "head"),
        P(None, "head"),
        P("head", None),
        P("seq", "head"),
        P("head", None, None),
    )
    return jax.shard_map(
        on_device,
        mesh=mesh,
        in_specs=placed,
        out_specs=(
            P("seq", "head"),
            P("seq", "head"),
            P("seq", "head"),
            P("seq", "head"),
            P("seq", "head"),
            P("head", "seq"),
            P("head", None, None),
        ),
        check_vma=False,
    )
```

```python
import jax
import jax.numpy as jnp
from jax import lax
from jax.sharding import PartitionSpec as P

DH = 128
BLOCK = 256


EPSILON = 1e-06
WIDE_TYPE = jnp.float32
HALF_TYPE = jnp.bfloat16


def causal_mask(width):
    return jnp.tril(jnp.ones((width, width), WIDE_TYPE)) > 0.5


def excl_prefix(states):
    running = jnp.cumsum(states, axis=0)
    return jnp.concatenate([jnp.zeros_like(states), running[:-1]], axis=0)


def excl_suffix(states):
    return jnp.flip(excl_prefix(jnp.flip(states, 0)), 0)


def flip(array, axis, bits):
    count = lax.axis_size(axis)
    return lax.ppermute(array, axis, [(rank, rank ^ bits) for rank in range(count)])


def bits_below(count):
    return [1 << place for place in range(count.bit_length() - 1)]


def spread(own, axis, lowest=1):
    blocks = {0: own}
    for bit in reversed([b for b in bits_below(lax.axis_size(axis)) if b >= lowest]):
        for k in sorted(blocks):
            blocks[k ^ bit] = flip(blocks[k], axis, bit)
    return blocks


def in_order(blocks, axis, width=1):
    rank = lax.axis_index(axis)
    whole = jnp.zeros((len(blocks),) + blocks[0].shape, blocks[0].dtype)
    for k, block in blocks.items():
        whole = lax.dynamic_update_slice(whole, block[None], ((rank ^ k) // width, 0, 0))
    return whole.reshape(-1, blocks[0].shape[1])


def piece(array, axis, k):
    rows = array.shape[0] // lax.axis_size(axis)
    return lax.dynamic_slice_in_dim(array, (lax.axis_index(axis) ^ k) * rows, rows, 0)


def pieces(terms, axis):
    return {k: piece(terms, axis, k) for k in range(lax.axis_size(axis))}


def halve(parts, axis, bit):
    made = None
    for k in sorted((k for k in parts if k & bit), reverse=True):
        moved = flip(parts.pop(k).astype(HALF_TYPE), axis, bit)
        if made is not None:
            moved, parts[made] = lax.optimization_barrier((moved, parts[made]))
        total = parts[k ^ bit].astype(WIDE_TYPE) + moved.astype(WIDE_TYPE)
        made = (k ^ bit) or None
        parts[k ^ bit] = total.astype(HALF_TYPE) if made else total
    return parts


def collect(parts, axis):
    for bit in bits_below(lax.axis_size(axis)):
        if any(k & bit for k in parts):
            parts = halve(parts, axis, bit)
    return parts[0]


def exchange(array, axis):
    count = lax.axis_size(axis)
    return {k: flip(piece(array, axis, k), axis, k) if k else piece(array, axis, 0) for k in range(count)}


def share(array, axis):
    count = lax.axis_size(axis)
    return {k: flip(array, axis, k) if k else array for k in range(count)}


def on_device(tokens, w_query, w_key, w_value, w_out, grad_out, state_in):
    row_count = tokens.shape[0]
    token_blocks = spread(tokens.T, "head")
    cot_own = grad_out.T
    cot_other = flip(cot_own, "head", 1)
    first = lax.axis_index("head") % 2 == 0
    cot_pair = jnp.concatenate(
        [jnp.where(first, cot_own, cot_other), jnp.where(first, cot_other, cot_own)]
    )
    ahead = [k for k in token_blocks if k and (not k & 1 or k < 4)]
    *arrived, cot_pair = lax.optimization_barrier(
        tuple(token_blocks[k] for k in ahead) + (cot_pair,)
    )
    for k, block in zip(ahead, arrived):
        token_blocks[k] = block
    gathered = in_order(token_blocks, "head")
    grad_full = in_order(spread(cot_pair, "head", 2), "head", 2)
    contract_first = (((0,), (0,)), ((), ()))
    contract_last = (((1,), (1,)), ((), ()))
    columns = w_query.shape[1]
    heads_here = columns // DH
    blocks = row_count // BLOCK
    block_shape = (blocks, BLOCK, heads_here, DH)
    query = (
        lax.dot_general(gathered, w_query, contract_first, preferred_element_type=WIDE_TYPE)
        .astype(HALF_TYPE)
        .reshape(block_shape)
    )
    keys = (
        lax.dot_general(gathered, w_key, contract_first, preferred_element_type=WIDE_TYPE)
        .astype(HALF_TYPE)
        .reshape(block_shape)
    )
    values = (
        lax.dot_general(gathered, w_value, contract_first, preferred_element_type=WIDE_TYPE)
        .astype(HALF_TYPE)
        .reshape(block_shape)
    )
    block_states = jnp.einsum("cshd,cshe->chde", keys, values, preferred_element_type=WIDE_TYPE)
    own_state = jnp.sum(block_states, axis=0)
    seq_rank = lax.axis_index("seq")
    every_state = share(own_state.astype(HALF_TYPE), "seq")
    before_dev = sum(
        jnp.where((seq_rank ^ k) < seq_rank, state.astype(WIDE_TYPE), 0.0)
        for k, state in every_state.items()
        if k
    )
    moved_input = exchange(gathered, "seq")
    prior_bf = (state_in[None] + before_dev[None] + excl_prefix(block_states)).astype(HALF_TYPE)
    allowed = causal_mask(BLOCK)[None, None]
    scores = jnp.einsum("cthd,cshd->chts", query, keys, preferred_element_type=WIDE_TYPE)
    scores_bf = jnp.where(allowed, scores, 0.0).astype(HALF_TYPE)
    mixed = jnp.einsum("chts,cshd->cthd", scores_bf, values, preferred_element_type=WIDE_TYPE)
    mixed = mixed + jnp.einsum("cthd,chde->cthe", query, prior_bf, preferred_element_type=WIDE_TYPE)
    inv_norm = lax.rsqrt(jnp.mean(mixed * mixed, axis=-1, keepdims=True) + EPSILON)
    normed = (mixed * inv_norm).astype(HALF_TYPE).reshape(row_count, columns)
    out_terms = lax.dot_general(
        w_out, normed, (((0,), (1,)), ((), ())), preferred_element_type=WIDE_TYPE
    )
    out_parts = halve(pieces(out_terms.astype(HALF_TYPE), "head"), "head", 1)
    out_parts, grad_full = lax.optimization_barrier((out_parts, grad_full))
    result = collect(out_parts, "head").astype(HALF_TYPE).T
    moved_cot = exchange(grad_full, "seq")
    grad_normed = lax.dot_general(
        grad_full, w_out, (((0,), (1,)), ((), ())), preferred_element_type=WIDE_TYPE
    ).reshape(block_shape)
    grad_mixed = inv_norm * (
        grad_normed
        - mixed * inv_norm * inv_norm * jnp.mean(grad_normed * mixed, axis=-1, keepdims=True)
    )
    grad_mixed = grad_mixed.astype(HALF_TYPE)
    back_states = jnp.einsum("cthd,cthe->chde", query, grad_mixed, preferred_element_type=WIDE_TYPE)
    own_back = jnp.sum(back_states, axis=0)
    every_back = {
        k: back.astype(WIDE_TYPE) for k, back in share(own_back.astype(HALF_TYPE), "seq").items()
    }
    after_dev = sum(
        jnp.where((seq_rank ^ k) > seq_rank, back, 0.0) for k, back in every_back.items() if k
    )
    in_rank = [
        sum(jnp.where((seq_rank ^ k) == owner, back, 0.0) for k, back in every_back.items())
        for owner in range(lax.axis_size("seq"))
    ]
    grad_state_in = sum(in_rank)
    later_bf = (after_dev[None] + excl_suffix(back_states)).astype(HALF_TYPE)
    grad_scores = jnp.einsum(
        "cthd,cshd->chts", grad_mixed, values, preferred_element_type=WIDE_TYPE
    )
    grad_scores = jnp.where(allowed, grad_scores, 0.0).astype(HALF_TYPE)
    grad_query = jnp.einsum("chts,cshd->cthd", grad_scores, keys, preferred_element_type=WIDE_TYPE)
    grad_query = grad_query + jnp.einsum(
        "cthe,chde->cthd", grad_mixed, prior_bf, preferred_element_type=WIDE_TYPE
    )
    grad_keys = jnp.einsum("chts,cthd->cshd", grad_scores, query, preferred_element_type=WIDE_TYPE)
    grad_keys = grad_keys + jnp.einsum(
        "cshe,chde->cshd", values, later_bf, preferred_element_type=WIDE_TYPE
    )
    grad_value = jnp.einsum(
        "chts,cthe->cshe", scores_bf, grad_mixed, preferred_element_type=WIDE_TYPE
    )
    grad_value = grad_value + jnp.einsum(
        "cshd,chde->cshe", keys, later_bf, preferred_element_type=WIDE_TYPE
    )
    grad_query = grad_query.astype(HALF_TYPE).reshape(row_count, columns)
    grad_keys = grad_keys.astype(HALF_TYPE).reshape(row_count, columns)
    grad_value = grad_value.astype(HALF_TYPE).reshape(row_count, columns)
    input_terms = lax.dot_general(
        w_query, grad_query, contract_last, preferred_element_type=WIDE_TYPE
    )
    input_terms = input_terms + lax.dot_general(
        w_key, grad_keys, contract_last, preferred_element_type=WIDE_TYPE
    )
    input_terms = input_terms + lax.dot_general(
        w_value, grad_value, contract_last, preferred_element_type=WIDE_TYPE
    )
    grad_tokens = collect(pieces(input_terms.astype(HALF_TYPE), "head"), "head").T
    all_grads = spread(jnp.concatenate([grad_query, grad_keys, grad_value, normed], axis=1), "seq")
    all_normed = {k: grads[:, 3 * columns :] for k, grads in all_grads.items()}
    grad_projections = sum(
        jnp.dot(moved_input[k], all_grads[k][:, : 3 * columns], preferred_element_type=WIDE_TYPE)
        for k in moved_input
    )
    grad_wq, grad_wk, grad_wv = jnp.split(grad_projections, 3, axis=1)
    grad_wo = sum(
        lax.dot_general(
            all_normed[k], moved_cot[k], (((0,), (1,)), ((), ())), preferred_element_type=WIDE_TYPE
        )
        for k in moved_cot
    )
    return (result, grad_tokens, grad_wq, grad_wk, grad_wv, grad_wo, grad_state_in)


def solution(mesh):
    placed = (
        P("seq", "head"),
        P(None, "head"),
        P(None, "head"),
        P(None, "head"),
        P("head", None),
        P("seq", "head"),
        P("head", None, None),
    )
    return jax.shard_map(
        on_device,
        mesh=mesh,
        in_specs=placed,
        out_specs=(
            P("seq", "head"),
            P("seq", "head"),
            P("seq", "head"),
            P("seq", "head"),
            P("seq", "head"),
            P("head", "seq"),
            P("head", None, None),
        ),
        check_vma=False,
    )
```
